32 devices in a mesh: tiles: 1, rows: 32 (over z, y, x, core).
Axes of the slice: x: 2, y: 2, z: 4, core: 2. Of those that a mesh axis runs over, the one named last changes fastest.
Arguments:
- features: bfloat16 [512, 512, 256], P(('tiles', 'rows')), may hold values from -6 to 6
- corners: int32 [256, 2], P(('tiles', 'rows')), may hold values from 0 to 511, as said below
- offsets: int32 [256, 1], P(('tiles', 'rows')), may hold values from 0 to 3; in each aligned block of 8 rows (0 to 7, 8 to 15, ...) at most 2 rows name the same one
- counts: int32 [32], P(('tiles', 'rows')), may hold values from 4 to 8, as said below
- classes: int32 [256], P(('tiles', 'rows')), may hold values from 0 to 14
- fpn_weight: bfloat16 [2304, 256], replicated, may hold values from -0.125 to 0.125
- head_weight: bfloat16 [2304, 256], replicated, may hold values from -0.125 to 0.125
- deconv_weight: bfloat16 [256, 1024], replicated, may hold values from -0.375 to 0.375
- class_weight: bfloat16 [15, 256], replicated, may hold values from -0.375 to 0.375
Outputs:
- masks: float32 [256, 1024], P(('tiles', 'rows'))
The draws below stay inside these ranges and needn't reach their ends.
Inputs may be any that keep to these rules, and one draw needn't show every extreme that they name: corners[q, 0] lies in owner q // 8's band of rows 16 (q // 8) .. 16 (q // 8 + 1) - 1; corners[q, 1] is at most 496. `offsets`: in each owner's 8 slots no offset occurs more than 2 times, and some offset occurs exactly 2 times. `counts`: some owner has all 8 slots live.
All inputs are finite; a program needn't handle non-finite values.
Results may differ from the reference program's by a relative error of at most 0.0051.
Values may be sent and summed in bfloat16 or wider, within the bound.
A program may use at most 192 MiB of HBM per device.

```python
import math
import jax
import jax.numpy as jnp
import numpy as np
from jax import lax

CHANNELS = 256
CLASSES = 15
ROWS_DEV = 16
COLS = 512
ROI_SIZE = 16
ROI_DEV = 8
WINDOW = 4
SLOTS = 2
MAP_ROWS = 512
ROIS = 256
HEAD_SLOTS = 256
MASK_CELLS = 1024
N_ROWS = 32


def draw_corners(key, part):
    key_rows = jax.random.fold_in(key, 11)
    key_cols = jax.random.fold_in(key, 12)
    owner = jnp.arange(ROIS, dtype=jnp.int32) // ROI_DEV
    rows_in = jax.random.randint(key_rows, (ROIS,), 0, ROWS_DEV, dtype=jnp.int32)
    cols_at = jax.random.randint(key_cols, (ROIS,), 0, COLS - ROI_SIZE + 1, dtype=jnp.int32)
    return jnp.stack([owner * ROWS_DEV + rows_in, cols_at], 1)


def draw_counts(key, part):
    key_counts = jax.random.fold_in(key, 21)
    key_full = jax.random.fold_in(key, 22)
    values = jax.random.randint(key_counts, (N_ROWS,), ROI_DEV // 2, ROI_DEV + 1, dtype=jnp.int32)
    fullest = jax.random.randint(key_full, (), 0, N_ROWS, dtype=jnp.int32)
    return jnp.where(jnp.arange(N_ROWS, dtype=jnp.int32) == fullest, ROI_DEV, values)


def place_ends(entries, own_key, smallest, high):
    extent = entries.shape
    index_at = [jax.random.randint(jax.random.fold_in(own_key, axis), (), 0, extent[axis]) for axis in range(len(extent))]
    entries = entries.at[tuple(index_at)].set(smallest)
    longest = extent.index(max(extent))
    index_at[longest] = (index_at[longest] + 1) % extent[longest]
    return entries.at[tuple(index_at)].set(high)


def levels(key, extent, split, smallest, top_value):
    def one(dim, shards_of):
        steps = jax.random.uniform(jax.random.fold_in(jax.random.fold_in(key, 6), dim), (shards_of,), jnp.float32, smallest / len(split), top_value / len(split))
        return jnp.repeat(jnp.exp(steps), extent[dim] // shards_of).reshape((-1,) + (1,) * (len(extent) - dim - 1))

    factor_of = one(*split[0])
    for cut in split[1:]:
        factor_of = factor_of * one(*cut)
    return factor_of


def shared_out(rng, own, number, rows, number_of, top, bound, skew):
    ranking = jax.random.permutation(rng, number_of)
    crowded, usual = portions_of(number_of, rows * top, bound, skew, True), portions_of(number_of, rows * top, bound, skew, False)
    places = jnp.arange(number_of)

    def named(lengths, offset_by):
        used = int((lengths > 0).sum())
        fixed = max(1, used // 4)
        moved = fixed + (places - fixed + offset_by * (used - fixed)) % max(1, number_of - fixed)
        return jnp.zeros((number_of,), jnp.int32).at[ranking[jnp.where(places < fixed, places, moved)]].set(jnp.asarray(lengths, jnp.int32))

    lengths = jnp.where(number % 4 == 0, named(crowded, number // 4), named(usual, number - number // 4 - 1))
    mixed = jax.random.permutation(jax.random.fold_in(own, 3), number_of)
    giver, receiver = mixed[0:number_of // 2 * 2:2], mixed[1:number_of // 2 * 2:2]
    margin = jnp.minimum(lengths[giver] - 1, bound - lengths[receiver]) // 2
    margin = jnp.where((giver == ranking[0]) | (receiver == ranking[0]) | (lengths[receiver] == 0), 0, jnp.maximum(margin, 0))
    moved = jax.random.randint(jax.random.fold_in(own, 4), (number_of // 2,), 0, 1 << 20) % (margin + 1)
    lengths = lengths.at[giver].add(-moved).at[receiver].add(moved)
    members = jnp.searchsorted(jnp.cumsum(lengths), jnp.arange(rows * top), side="right").astype(jnp.int32)
    listing = members.reshape(top, rows).T
    listing = listing[jax.random.permutation(jax.random.fold_in(own, 1), rows)]
    offset_by = jax.random.randint(jax.random.fold_in(own, 2), (rows, 1), 0, top)
    return jnp.take_along_axis(listing, (jnp.arange(top)[None, :] + offset_by) % top, axis=1)


def portions_of(amount, total, reach, lean, full):
    portions = [(1 << 20) // math.isqrt(standing ** lean) + 1 for standing in range(1, amount + 1)]
    largest = reach if full else min(reach, max(-(-total // amount), total * portions[0] // sum(portions)))
    least = 1 if total - largest >= amount - 1 else 0
    given, rest = [largest] + [least] * (amount - 1), total - largest - least * (amount - 1)
    while rest > 0:
        movable = [i for i in range(1, amount) if given[i] < largest] or [i for i in range(1, amount) if given[i] < reach]
        mass, left = sum([portions[i] for i in movable]), rest
        for i in movable:
            addition = min(reach - given[i], max(1, left * portions[i] // mass), rest)
            given[i] = given[i] + addition
            rest = rest - addition
    return np.array(given)


def scatter_about(rng, shape, scale, bound, cuts=(), kind=jnp.bfloat16):
    level = levels(rng, shape, cuts, -0.22, 0.18) if cuts else 1.0
    entries = jax.random.normal(rng, shape, jnp.float32) * scale * level
    return jnp.minimum(jnp.maximum(entries, -bound), bound).astype(kind)


def setup_inputs(seed: int = 0, part: int = 0) -> dict:
    keys = jax.random.split(jax.random.key(seed), 10)
    part_keys = jax.random.split(jax.random.fold_in(keys[9], part), 10)
    features = scatter_about(part_keys[0], (MAP_ROWS, COLS, CHANNELS), 1.0, 6.0, ((0, 32),))
    corners = draw_corners(jax.random.fold_in(jax.random.fold_in(keys[9], part), 71), part)
    offsets_keys = jax.random.split(jax.random.fold_in(part_keys[2], 1), ROIS // ROI_DEV)
    offsets_turns = jax.random.permutation(jax.random.fold_in(part_keys[2], 3), ROIS // ROI_DEV)
    offsets = jax.vmap(lambda own, number: shared_out(jax.random.fold_in(part_keys[2], 2), own, number, ROI_DEV, WINDOW, 1, SLOTS, 1))(offsets_keys, offsets_turns).reshape((ROIS, 1))
    counts = draw_counts(jax.random.fold_in(jax.random.fold_in(keys[9], part), 71), part)
    classes = place_ends(jax.random.randint(part_keys[4], (ROIS,), 0, CLASSES), jax.random.fold_in(part_keys[4], 1), 0, CLASSES - 1).astype(jnp.int32)
    fpn_weight = scatter_about(keys[5], (9 * CHANNELS, CHANNELS), (9 * CHANNELS) ** -0.5, 0.125)
    head_weight = scatter_about(keys[6], (9 * CHANNELS, CHANNELS), (9 * CHANNELS) ** -0.5, 0.125)
    deconv_weight = scatter_about(keys[7], (CHANNELS, 4 * CHANNELS), CHANNELS ** -0.5, 0.375)
    class_weight = scatter_about(keys[8], (CLASSES, CHANNELS), CHANNELS ** -0.5, 0.375)
    return dict(features=features, corners=corners, offsets=offsets, counts=counts, classes=classes, fpn_weight=fpn_weight, head_weight=head_weight, deconv_weight=deconv_weight, class_weight=class_weight)


def conv_taps(padded, weights):
    chans = padded.shape[-1]
    height = padded.shape[-3] - 2
    width = padded.shape[-2] - 2
    total = jnp.zeros(padded.shape[:-3] + (height, width, weights.shape[1]), jnp.float32)
    for tap in range(9):
        row_off = tap // 3
        col_off = tap % 3
        window = padded[..., row_off:row_off + height, col_off:col_off + width, :].astype(jnp.float32)
        piece = weights[tap * chans:(tap + 1) * chans].astype(jnp.float32)
        total = total + jnp.einsum("...c,cd->...d", window, piece, precision=lax.Precision.HIGHEST)
    return total


def mask_head(blocks, class_ids, head_weight, deconv_weight, class_weight):
    count, side, _, chans = blocks.shape
    padded = jnp.pad(blocks, ((0, 0), (1, 1), (1, 1), (0, 0)))
    hidden = jax.nn.relu(conv_taps(padded, head_weight)).astype(jnp.bfloat16)
    upsampled = jnp.einsum("bhwc,ck->bhwk", hidden.astype(jnp.float32), deconv_weight.astype(jnp.float32), precision=lax.Precision.HIGHEST)
    upsampled = jax.nn.relu(upsampled).astype(jnp.bfloat16).reshape(count, side, side, 2, 2, chans)
    chosen = class_weight[class_ids].astype(jnp.float32)
    logit = jnp.einsum("bhwyxc,bc->bhwyx", upsampled.astype(jnp.float32), chosen, precision=lax.Precision.HIGHEST)
    return logit.transpose(0, 1, 3, 2, 4).reshape(count, 4 * side * side)


def reference(features, corners, offsets, counts, classes, fpn_weight, head_weight, deconv_weight, class_weight):
    padded = jnp.pad(features, ((1, 1), (1, 1), (0, 0)))
    pyramid = conv_taps(padded, fpn_weight).astype(jnp.bfloat16)
    extended = jnp.concatenate([pyramid, jnp.zeros((ROI_SIZE - 1, COLS, CHANNELS), jnp.bfloat16)], 0)

    def crop(row_at, col_at):
        return lax.dynamic_slice(extended, (row_at, col_at, jnp.int32(0)), (ROI_SIZE, ROI_SIZE, CHANNELS))

    def per_owner(args):
        tops, lefts, class_ids = args
        blocks = jax.vmap(crop)(tops, lefts)
        return mask_head(blocks, class_ids, head_weight, deconv_weight, class_weight)

    logits = lax.map(per_owner, (corners[:, 0].astype(jnp.int32).reshape(N_ROWS, ROI_DEV),
                                 corners[:, 1].astype(jnp.int32).reshape(N_ROWS, ROI_DEV),
                                 classes.reshape(N_ROWS, ROI_DEV)))
    logits = logits.reshape(ROIS, MASK_CELLS)
    ordinal = jnp.arange(ROIS, dtype=jnp.int32)
    owner = ordinal // ROI_DEV
    local = ordinal % ROI_DEV
    valid = local < counts[owner]
    target = offsets[:, 0].astype(jnp.int32)
    target2 = target.reshape(N_ROWS, ROI_DEV)
    valid2 = valid.reshape(N_ROWS, ROI_DEV)
    slot_ids = jnp.arange(ROI_DEV, dtype=jnp.int32)
    earlier = (target2[:, :, None] == target2[:, None, :]) & valid2[:, None, :] & (slot_ids[None, :] < slot_ids[:, None])[None]
    rank = jnp.sum(earlier.astype(jnp.int32), -1).reshape(ROIS)
    head = (owner + target) % N_ROWS
    row_of = jnp.where(valid, head * (WINDOW * SLOTS) + target * SLOTS + rank, HEAD_SLOTS).astype(jnp.int32)
    masks = jnp.zeros((HEAD_SLOTS, MASK_CELLS), jnp.float32).at[row_of].set(logits, mode="drop")
    return masks
```

```python
import functools

import jax
import jax.numpy as jnp
from jax import lax
from jax.experimental import pallas as pl
from jax.experimental.pallas import tpu as pltpu
from jax.sharding import PartitionSpec as P

SIDE = 16
WINDOW = 4
SLOTS = 2
EDGE = 16
GROUP = 2
MESH = pl.DeviceIdType.MESH


def kernel(
    count,
    meta_sm,
    meta_vm,
    feat,
    fpn_hbm,
    head_hbm,
    dec_hbm,
    cls_w,
    out,
    band,
    wide,
    fpn_w,
    head_w,
    dec_w,
    above_row,
    near_vm,
    near_sm,
    sent,
    got,
    ends,
    joined,
    wins,
    blocks,
    logits,
    outgoing,
    incoming,
    load_sem,
    small_send,
    small_recv,
    piece_send,
    piece_recv,
    mask_send,
    mask_recv,
):
    me = lax.axis_index("rows")
    rois = sent.shape[0]
    band_rows, columns, chans = band.shape
    has_up = me > 0
    has_down = me < count - 1

    def at(step):
        return {"rows": lax.rem(me + step + count, count)}

    barrier = pltpu.get_barrier_semaphore()
    for step in range(1, WINDOW):
        for sign in (1, -1):
            pl.semaphore_signal(barrier, inc=1, device_id=at(sign * step), device_id_type=MESH)

    loads = [
        pltpu.make_async_copy(feat, band, load_sem.at[0]),
        pltpu.make_async_copy(fpn_hbm, fpn_w, load_sem.at[1]),
        pltpu.make_async_copy(head_hbm, head_w, load_sem.at[2]),
        pltpu.make_async_copy(dec_hbm, dec_w, load_sem.at[3]),
    ]
    for load in loads:
        load.start()

    halves = wide.shape[0]
    lanes = wide.shape[-1]
    wide[:, :, 0:EDGE, :] = jnp.zeros((halves, band_rows + 1, EDGE, lanes), jnp.float32)
    wide[:, :, EDGE + columns :, :] = jnp.zeros((halves, band_rows + 1, EDGE, lanes), jnp.float32)
    blocks[...] = jnp.zeros_like(blocks)

    pl.semaphore_wait(barrier, 2 * (WINDOW - 1))

    corners_up = pltpu.make_async_remote_copy(
        src_ref=meta_vm,
        dst_ref=near_vm,
        send_sem=small_send.at[0],
        recv_sem=small_recv.at[0],
        device_id=at(1),
        device_id_type=MESH,
    )
    last_row = pltpu.make_async_remote_copy(
        src_ref=band.at[pl.ds(band_rows - 1, 1)],
        dst_ref=above_row,
        send_sem=small_send.at[1],
        recv_sem=small_recv.at[1],
        device_id=at(1),
        device_id_type=MESH,
    )

    @pl.when(has_down)
    def _():
        corners_up.start()

    loads[0].wait()

    @pl.when(has_down)
    def _():
        last_row.start()

    def widen(i, carry):
        for h in range(halves):
            wide[h, pl.ds(i + 1, 1), EDGE : EDGE + columns, :] = band[
                pl.ds(i, 1), :, h * lanes : (h + 1) * lanes
            ].astype(jnp.float32)
        return carry

    lax.fori_loop(0, band_rows, widen, 0)

    def piece(q):
        return pltpu.make_async_remote_copy(
            src_ref=sent.at[q],
            dst_ref=got.at[q],
            send_sem=piece_send.at[q],
            recv_sem=piece_recv.at[q],
            device_id=at(-1),
            device_id_type=MESH,
        )

    @pl.when(has_up)
    def _():
        corners_up.wait_recv()
        near = pltpu.make_async_copy(near_vm, near_sm, load_sem.at[4])
        near.start()
        near.wait()

        def gather(q, carry):
            start = near_sm[q, 1] + (EDGE - 1)
            for h in range(halves):
                part = slice(h * lanes, (h + 1) * lanes)
                for i in range(band_rows):
                    sent[q, i, :, part] = wide[h, i + 1, pl.ds(start + 1, SIDE), :].astype(
                        jnp.bfloat16
                    )
                    ends[0, i : i + 1, part] = wide[h, i + 1, pl.ds(start, 1), :]
                    ends[1, i : i + 1, part] = wide[h, i + 1, pl.ds(start + SIDE + 1, 1), :]
            sent[q, SIDE:] = ends[...].astype(jnp.bfloat16)
            piece(q).start()
            return carry

        lax.fori_loop(0, rois, gather, 0)
        last_row.wait_recv()
        for h in range(halves):
            wide[h, 0:1, EDGE : EDGE + columns, :] = above_row[
                :, :, h * lanes : (h + 1) * lanes
            ].astype(jnp.float32)

    @pl.when(jnp.logical_not(has_up))
    def _():
        wide[:, 0:1, EDGE : EDGE + columns, :] = jnp.zeros((halves, 1, columns, lanes), jnp.float32)

    def own(q, carry):
        start = meta_sm[q, 1] + (EDGE - 1)
        for dj in range(3):
            for h in range(halves):
                for i in range(band_rows + 1):
                    wins[q, dj, i, :, h * lanes : (h + 1) * lanes] = wide[
                        h, i, pl.ds(start + dj, SIDE), :
                    ].astype(jnp.bfloat16)
        return carry

    lax.fori_loop(0, rois, own, 0)

    @pl.when(jnp.logical_not(has_down))
    def _():
        got[...] = jnp.zeros_like(got)

    for load in loads[1:]:
        load.wait()

    limit = jnp.where(has_down, 2 * band_rows, band_rows)

    def group(g, carry):
        base = g * GROUP
        for u in range(GROUP):
            q = base + u

            @pl.when(has_down)
            def _():
                piece(q).wait_recv()

            joined[:, 8 : 8 + SIDE, :] = got[q, 0:SIDE].astype(jnp.float32)
            ends[...] = got[q, SIDE:].astype(jnp.float32)
            for i in range(band_rows):
                joined[i, 7:8, :] = ends[0, i : i + 1, :]
                joined[i, 8 + SIDE : 9 + SIDE, :] = ends[1, i : i + 1, :]
            for dj in range(3):
                wins[q, dj, band_rows + 1 :] = joined[:, 7 + dj : 7 + dj + SIDE, :].astype(
                    jnp.bfloat16
                )
        tops = [lax.rem(meta_sm[base + u, 0], band_rows) for u in range(GROUP)]
        total = None
        for tap in range(9):
            di, dj = tap // 3, tap % 3
            lhs = jnp.concatenate(
                [
                    wins[base + u, dj, pl.ds(tops[u] + di, SIDE)].reshape(SIDE * SIDE, chans)
                    for u in range(GROUP)
                ],
                axis=0,
            )
            term = jnp.dot(
                lhs, fpn_w[tap * chans : (tap + 1) * chans], preferred_element_type=jnp.float32
            )
            total = term if total is None else total + term
        total = total.reshape(GROUP, SIDE, SIDE, chans)
        row = lax.broadcasted_iota(jnp.int32, (SIDE, SIDE, chans), 0)
        for u in range(GROUP):
            kept = jnp.where(row + tops[u] < limit, total[u], 0.0)
            blocks[u, 1 : 1 + SIDE, 8 : 8 + SIDE, :] = kept
        total = None
        for tap in range(9):
            di, dj = tap // 3, tap % 3
            lhs = (
                blocks[:, di : di + SIDE, 7 + dj : 7 + dj + SIDE, :]
                .astype(jnp.bfloat16)
                .reshape(GROUP * SIDE * SIDE, chans)
            )
            term = jnp.dot(
                lhs, head_w[tap * chans : (tap + 1) * chans], preferred_element_type=jnp.float32
            )
            total = term if total is None else total + term
        hidden = jnp.maximum(total, 0.0).astype(jnp.bfloat16)
        for yx in range(4):
            up = jnp.dot(
                hidden, dec_w[:, yx * chans : (yx + 1) * chans], preferred_element_type=jnp.float32
            )
            up = jnp.maximum(up, 0.0).astype(jnp.bfloat16)
            every = lax.dot_general(
                cls_w[...], up, (((1,), (1,)), ((), ())), preferred_element_type=jnp.float32
            )
            which = lax.broadcasted_iota(jnp.int32, (every.shape[0], SIDE * SIDE), 0)
            for u in range(GROUP):
                mine = every[:, u * SIDE * SIDE : (u + 1) * SIDE * SIDE]
                logits[base + u, yx : yx + 1, :] = jnp.sum(
                    jnp.where(which == meta_sm[base + u, 3], mine, 0.0), axis=0, keepdims=True
                )
        return carry

    lax.fori_loop(0, rois // GROUP, group, 0)

    slots = []
    for q in range(rois):
        rank = jnp.int32(0)
        for p in range(q):
            same = (meta_sm[p, 2] == meta_sm[q, 2]) & (p < meta_sm[p, 4])
            rank = rank + same.astype(jnp.int32)
        slots.append(jnp.where(q < meta_sm[q, 4], meta_sm[q, 2] * SLOTS + rank, WINDOW * SLOTS))

    def mask(f):
        return pltpu.make_async_remote_copy(
            src_ref=outgoing.at[f],
            dst_ref=incoming.at[f],
            send_sem=mask_send.at[f],
            recv_sem=mask_recv.at[f],
            device_id=at(f),
            device_id_type=MESH,
        )

    for f in range(WINDOW - 1, -1, -1):
        for k in range(SLOTS):
            held = jnp.zeros(logits.shape[1:], jnp.float32)
            for q in range(rois):
                held = jnp.where(slots[q] == f * SLOTS + k, logits[q], held)
            if f:
                outgoing[f, k] = held
            else:
                out[k] = held
        if f:
            mask(f).start()

    for f in range(1, WINDOW):
        mask(f).wait_recv()
        out[f * SLOTS : (f + 1) * SLOTS] = incoming[f]

    for f in range(1, WINDOW):
        mask(f).wait_send()

    @pl.when(has_down)
    def _():
        corners_up.wait_send()
        last_row.wait_send()

    @pl.when(has_up)
    def _():
        def drain(q, carry):
            piece(q).wait_send()
            return carry

        lax.fori_loop(0, rois, drain, 0)


def body(
    count,
    features,
    corners,
    offsets,
    counts,
    classes,
    fpn_weight,
    head_weight,
    deconv_weight,
    class_weight,
):
    band_rows, columns, chans = features.shape
    rois = corners.shape[0]
    meta = jnp.concatenate(
        [corners, offsets, classes[:, None], jnp.broadcast_to(counts[:, None], (rois, 1))], 1
    )
    meta = jnp.pad(meta, ((0, 0), (0, 128 - meta.shape[1])))
    cls = class_weight
    vmem = pl.BlockSpec(memory_space=pltpu.VMEM)
    anyw = pl.BlockSpec(memory_space=pl.ANY)
    bf16, f32 = jnp.bfloat16, jnp.float32
    cells = SIDE * SIDE
    masks = pl.pallas_call(
        functools.partial(kernel, count),
        out_shape=jax.ShapeDtypeStruct((WINDOW * SLOTS, 4, cells), f32),
        in_specs=[pl.BlockSpec(memory_space=pltpu.SMEM), vmem, anyw, anyw, anyw, anyw, vmem],
        out_specs=vmem,
        scratch_shapes=[
            pltpu.VMEM(features.shape, bf16),
            pltpu.VMEM((chans // 128, band_rows + 1, columns + 2 * EDGE, 128), f32),
            pltpu.VMEM(fpn_weight.shape, bf16),
            pltpu.VMEM(head_weight.shape, bf16),
            pltpu.VMEM(deconv_weight.shape, bf16),
            pltpu.VMEM((1, columns, chans), bf16),
            pltpu.VMEM((rois, 128), jnp.int32),
            pltpu.SMEM((rois, 128), jnp.int32),
            pltpu.VMEM((rois, SIDE + 2, SIDE, chans), bf16),
            pltpu.VMEM((rois, SIDE + 2, SIDE, chans), bf16),
            pltpu.VMEM((2, SIDE, chans), f32),
            pltpu.VMEM((SIDE, 2 * SIDE, chans), f32),
            pltpu.VMEM((rois, 3, 2 * band_rows + 1, SIDE, chans), bf16),
            pltpu.VMEM((GROUP, SIDE + 2, 2 * SIDE, chans), f32),
            pltpu.VMEM((rois, 4, cells), f32),
            pltpu.VMEM((WINDOW, SLOTS, 4, cells), f32),
            pltpu.VMEM((WINDOW, SLOTS, 4, cells), f32),
            pltpu.SemaphoreType.DMA((5,)),
            pltpu.SemaphoreType.DMA((2,)),
            pltpu.SemaphoreType.DMA((2,)),
            pltpu.SemaphoreType.DMA((rois,)),
            pltpu.SemaphoreType.DMA((rois,)),
            pltpu.SemaphoreType.DMA((WINDOW,)),
            pltpu.SemaphoreType.DMA((WINDOW,)),
        ],
        compiler_params=pltpu.CompilerParams(collective_id=0, has_side_effects=True),
    )(meta, meta, features, fpn_weight, head_weight, deconv_weight, cls)
    masks = masks.reshape(WINDOW * SLOTS, 2, 2, SIDE, SIDE)
    return masks.transpose(0, 3, 1, 4, 2).reshape(WINDOW * SLOTS, 4 * cells)


def solution(mesh):
    placed = (
        P(("tiles", "rows"), None, None),
        P(("tiles", "rows"), None),
        P(("tiles", "rows"), None),
        P(("tiles", "rows")),
        P(("tiles", "rows")),
        P(),
        P(),
        P(),
        P(),
    )
    return jax.shard_map(
        functools.partial(body, mesh.shape["rows"]),
        mesh=mesh,
        in_specs=placed,
        out_specs=P(("tiles", "rows"), None),
        check_vma=False,
    )
```

```python
import functools

import jax
import jax.numpy as jnp
from jax import lax
from jax.experimental import pallas as pl
from jax.experimental.pallas import tpu as pltpu
from jax.sharding import PartitionSpec as P

SIDE = 16
WINDOW = 4
SLOTS = 2
EDGE = 16
GROUP = 2
MESH = pl.DeviceIdType.MESH


def kernel(
    count,
    corners_sm,
    corners_vm,
    offset_sm,
    count_sm,
    class_sm,
    feat,
    fpn_hbm,
    head_hbm,
    dec_hbm,
    cls_w,
    out,
    band,
    wide,
    fpn_w,
    head_w,
    dec_w,
    above_row,
    near_vm,
    near_sm,
    sent,
    got,
    ends,
    joined,
    wins,
    blocks,
    logits,
    outgoing,
    incoming,
    load_sem,
    small_send,
    small_recv,
    piece_send,
    piece_recv,
    mask_send,
    mask_recv,
):
    me = lax.axis_index("rows")
    rois = sent.shape[0]
    band_rows, columns, chans = band.shape
    has_up = me > 0
    has_down = me < count - 1

    def at(step):
        return {"rows": lax.rem(me + step + count, count)}

    barrier = pltpu.get_barrier_semaphore()
    for step in range(1, WINDOW):
        for sign in (1, -1):
            pl.semaphore_signal(barrier, inc=1, device_id=at(sign * step), device_id_type=MESH)

    loads = [
        pltpu.make_async_copy(feat, band, load_sem.at[0]),
        pltpu.make_async_copy(fpn_hbm, fpn_w, load_sem.at[1]),
        pltpu.make_async_copy(head_hbm, head_w, load_sem.at[2]),
        pltpu.make_async_copy(dec_hbm, dec_w, load_sem.at[3]),
    ]
    for load in loads:
        load.start()

    halves = wide.shape[0]
    lanes = wide.shape[-1]
    wide[:, :, 0:EDGE, :] = jnp.zeros((halves, band_rows + 1, EDGE, lanes), jnp.float32)
    wide[:, :, EDGE + columns :, :] = jnp.zeros((halves, band_rows + 1, EDGE, lanes), jnp.float32)
    blocks[...] = jnp.zeros_like(blocks)

    pl.semaphore_wait(barrier, 2 * (WINDOW - 1))

    corners_up = pltpu.make_async_remote_copy(
        src_ref=corners_vm,
        dst_ref=near_vm,
        send_sem=small_send.at[0],
        recv_sem=small_recv.at[0],
        device_id=at(1),
        device_id_type=MESH,
    )
    last_row = pltpu.make_async_remote_copy(
        src_ref=feat.at[pl.ds(band_rows - 1, 1)],
        dst_ref=above_row,
        send_sem=small_send.at[1],
        recv_sem=small_recv.at[1],
        device_id=at(1),
        device_id_type=MESH,
    )

    @pl.when(has_down)
    def _():
        corners_up.start()
        last_row.start()

    loads[0].wait()

    def widen(i, carry):
        for h in range(halves):
            wide[h, pl.ds(i + 1, 1), EDGE : EDGE + columns, :] = band[
                pl.ds(i, 1), :, h * lanes : (h + 1) * lanes
            ].astype(jnp.float32)
        return carry

    lax.fori_loop(0, band_rows, widen, 0)

    def piece(q):
        return pltpu.make_async_remote_copy(
            src_ref=sent.at[q],
            dst_ref=got.at[q],
            send_sem=piece_send.at[q],
            recv_sem=piece_recv.at[q],
            device_id=at(-1),
            device_id_type=MESH,
        )

    @pl.when(has_up)
    def _():
        corners_up.wait_recv()
        near = pltpu.make_async_copy(near_vm, near_sm, load_sem.at[4])
        near.start()
        near.wait()

        def gather(q, carry):
            start = near_sm[1, q] + (EDGE - 1)
            for h in range(halves):
                part = slice(h * lanes, (h + 1) * lanes)
                for i in range(band_rows):
                    sent[q, i, :, part] = wide[h, i + 1, pl.ds(start + 1, SIDE), :].astype(
                        jnp.bfloat16
                    )
                    ends[0, i : i + 1, part] = wide[h, i + 1, pl.ds(start, 1), :]
                    ends[1, i : i + 1, part] = wide[h, i + 1, pl.ds(start + SIDE + 1, 1), :]
            sent[q, SIDE:] = ends[...].astype(jnp.bfloat16)
            piece(q).start()
            return carry

        lax.fori_loop(0, rois, gather, 0)
        last_row.wait_recv()
        for h in range(halves):
            wide[h, 0:1, EDGE : EDGE + columns, :] = above_row[
                :, :, h * lanes : (h + 1) * lanes
            ].astype(jnp.float32)

    @pl.when(jnp.logical_not(has_up))
    def _():
        wide[:, 0:1, EDGE : EDGE + columns, :] = jnp.zeros((halves, 1, columns, lanes), jnp.float32)

    def own(q, carry):
        start = corners_sm[1, q] + (EDGE - 1)
        for dj in range(3):
            for h in range(halves):
                for i in range(band_rows + 1):
                    wins[q, dj, i, :, h * lanes : (h + 1) * lanes] = wide[
                        h, i, pl.ds(start + dj, SIDE), :
                    ].astype(jnp.bfloat16)
        return carry

    lax.fori_loop(0, rois, own, 0)

    @pl.when(jnp.logical_not(has_down))
    def _():
        got[...] = jnp.zeros_like(got)

    for load in loads[1:]:
        load.wait()

    limit = jnp.where(has_down, 2 * band_rows, band_rows)

    def group(g, carry):
        base = g * GROUP
        for u in range(GROUP):
            q = base + u

            @pl.when(has_down)
            def _():
                piece(q).wait_recv()

            joined[:, 8 : 8 + SIDE, :] = got[q, 0:SIDE].astype(jnp.float32)
            ends[...] = got[q, SIDE:].astype(jnp.float32)
            for i in range(band_rows):
                joined[i, 7:8, :] = ends[0, i : i + 1, :]
                joined[i, 8 + SIDE : 9 + SIDE, :] = ends[1, i : i + 1, :]
            for dj in range(3):
                wins[q, dj, band_rows + 1 :] = joined[:, 7 + dj : 7 + dj + SIDE, :].astype(
                    jnp.bfloat16
                )
        tops = [lax.rem(corners_sm[0, base + u], band_rows) for u in range(GROUP)]
        total = None
        for tap in range(9):
            di, dj = tap // 3, tap % 3
            lhs = jnp.concatenate(
                [
                    wins[base + u, dj, pl.ds(tops[u] + di, SIDE)].reshape(SIDE * SIDE, chans)
                    for u in range(GROUP)
                ],
                axis=0,
            )
            term = jnp.dot(
                lhs, fpn_w[tap * chans : (tap + 1) * chans], preferred_element_type=jnp.float32
            )
            total = term if total is None else total + term
        total = total.reshape(GROUP, SIDE, SIDE, chans)
        row = lax.broadcasted_iota(jnp.int32, (SIDE, SIDE, chans), 0)
        for u in range(GROUP):
            kept = jnp.where(row + tops[u] < limit, total[u], 0.0)
            blocks[u, 1 : 1 + SIDE, 8 : 8 + SIDE, :] = kept
        total = None
        for tap in range(9):
            di, dj = tap // 3, tap % 3
            lhs = (
                blocks[:, di : di + SIDE, 7 + dj : 7 + dj + SIDE, :]
                .astype(jnp.bfloat16)
                .reshape(GROUP * SIDE * SIDE, chans)
            )
            term = jnp.dot(
                lhs, head_w[tap * chans : (tap + 1) * chans], preferred_element_type=jnp.float32
            )
            total = term if total is None else total + term
        hidden = jnp.maximum(total, 0.0).astype(jnp.bfloat16)
        for yx in range(4):
            up = jnp.dot(
                hidden, dec_w[:, yx * chans : (yx + 1) * chans], preferred_element_type=jnp.float32
            )
            up = jnp.maximum(up, 0.0).astype(jnp.bfloat16)
            every = lax.dot_general(
                cls_w[...], up, (((1,), (1,)), ((), ())), preferred_element_type=jnp.float32
            )
            which = lax.broadcasted_iota(jnp.int32, (every.shape[0], SIDE * SIDE), 0)
            for u in range(GROUP):
                mine = every[:, u * SIDE * SIDE : (u + 1) * SIDE * SIDE]
                logits[base + u, yx : yx + 1, :] = jnp.sum(
                    jnp.where(which == class_sm[base + u], mine, 0.0), axis=0, keepdims=True
                )
        return carry

    lax.fori_loop(0, rois // GROUP, group, 0)

    slots = []
    for q in range(rois):
        rank = jnp.int32(0)
        for p in range(q):
            same = (offset_sm[p] == offset_sm[q]) & (p < count_sm[0])
            rank = rank + same.astype(jnp.int32)
        slots.append(jnp.where(q < count_sm[0], offset_sm[q] * SLOTS + rank, WINDOW * SLOTS))

    def mask(f):
        return pltpu.make_async_remote_copy(
            src_ref=outgoing.at[f],
            dst_ref=incoming.at[f],
            send_sem=mask_send.at[f],
            recv_sem=mask_recv.at[f],
            device_id=at(f),
            device_id_type=MESH,
        )

    for f in range(WINDOW - 1, -1, -1):
        for k in range(SLOTS):
            held = jnp.zeros(logits.shape[1:], jnp.float32)
            for q in range(rois):
                held = jnp.where(slots[q] == f * SLOTS + k, logits[q], held)
            if f:
                outgoing[f, k] = held
            else:
                out[k] = held
        if f:
            mask(f).start()

    for f in range(1, WINDOW):
        mask(f).wait_recv()
        out[f * SLOTS : (f + 1) * SLOTS] = incoming[f]

    for f in range(1, WINDOW):
        mask(f).wait_send()

    @pl.when(has_down)
    def _():
        corners_up.wait_send()
        last_row.wait_send()

    @pl.when(has_up)
    def _():
        def drain(q, carry):
            piece(q).wait_send()
            return carry

        lax.fori_loop(0, rois, drain, 0)


def body(
    count,
    features,
    corners,
    offsets,
    counts,
    classes,
    fpn_weight,
    head_weight,
    deconv_weight,
    class_weight,
):
    band_rows, columns, chans = features.shape
    rois = corners.shape[0]
    spots = corners.T
    smem = pl.BlockSpec(memory_space=pltpu.SMEM)
    cls = class_weight
    vmem = pl.BlockSpec(memory_space=pltpu.VMEM)
    anyw = pl.BlockSpec(memory_space=pl.ANY)
    bf16, f32 = jnp.bfloat16, jnp.float32
    cells = SIDE * SIDE
    masks = pl.pallas_call(
        functools.partial(kernel, count),
        out_shape=jax.ShapeDtypeStruct((WINDOW * SLOTS, 4, cells), f32),
        in_specs=[smem, vmem, smem, smem, smem, anyw, anyw, anyw, anyw, vmem],
        out_specs=vmem,
        scratch_shapes=[
            pltpu.VMEM(features.shape, bf16),
            pltpu.VMEM((chans // 128, band_rows + 1, columns + 2 * EDGE, 128), f32),
            pltpu.VMEM(fpn_weight.shape, bf16),
            pltpu.VMEM(head_weight.shape, bf16),
            pltpu.VMEM(deconv_weight.shape, bf16),
            pltpu.VMEM((1, columns, chans), bf16),
            pltpu.VMEM(spots.shape, jnp.int32),
            pltpu.SMEM(spots.shape, jnp.int32),
            pltpu.VMEM((rois, SIDE + 2, SIDE, chans), bf16),
            pltpu.VMEM((rois, SIDE + 2, SIDE, chans), bf16),
            pltpu.VMEM((2, SIDE, chans), f32),
            pltpu.VMEM((SIDE, 2 * SIDE, chans), f32),
            pltpu.VMEM((rois, 3, 2 * band_rows + 1, SIDE, chans), bf16),
            pltpu.VMEM((GROUP, SIDE + 2, 2 * SIDE, chans), f32),
            pltpu.VMEM((rois, 4, cells), f32),
            pltpu.VMEM((WINDOW, SLOTS, 4, cells), f32),
            pltpu.VMEM((WINDOW, SLOTS, 4, cells), f32),
            pltpu.SemaphoreType.DMA((5,)),
            pltpu.SemaphoreType.DMA((2,)),
            pltpu.SemaphoreType.DMA((2,)),
            pltpu.SemaphoreType.DMA((rois,)),
            pltpu.SemaphoreType.DMA((rois,)),
            pltpu.SemaphoreType.DMA((WINDOW,)),
            pltpu.SemaphoreType.DMA((WINDOW,)),
        ],
        compiler_params=pltpu.CompilerParams(collective_id=0, has_side_effects=True),
    )(
        spots,
        spots,
        offsets.reshape(rois),
        counts,
        classes,
        features,
        fpn_weight,
        head_weight,
        deconv_weight,
        cls,
    )
    masks = masks.reshape(WINDOW * SLOTS, 2, 2, SIDE, SIDE)
    return masks.transpose(0, 3, 1, 4, 2).reshape(WINDOW * SLOTS, 4 * cells)


def solution(mesh):
    placed = (
        P(("tiles", "rows"), None, None),
        P(("tiles", "rows"), None),
        P(("tiles", "rows"), None),
        P(("tiles", "rows")),
        P(("tiles", "rows")),
        P(),
        P(),
        P(),
        P(),
    )
    return jax.shard_map(
        functools.partial(body, mesh.shape["rows"]),
        mesh=mesh,
        in_specs=placed,
        out_specs=P(("tiles", "rows"), None),
        check_vma=False,
    )
```

```python
import functools

import jax
import jax.numpy as jnp
from jax import lax
from jax.experimental import pallas as pl
from jax.experimental.pallas import tpu as pltpu
from jax.sharding import PartitionSpec as P

SIDE = 16
WINDOW = 4
SLOTS = 2
EDGE = 16
GROUP = 2
MESH = pl.DeviceIdType.MESH


def kernel(
    count,
    corners_sm,
    corners_vm,
    offset_sm,
    count_sm,
    class_sm,
    feat,
    fpn_hbm,
    head_hbm,
    dec_hbm,
    cls_w,
    out,
    band,
    wide,
    fpn_w,
    head_w,
    dec_w,
    above_row,
    near_vm,
    near_sm,
    sent,
    got,
    ends,
    joined,
    wins,
    blocks,
    logits,
    outgoing,
    incoming,
    load_sem,
    small_send,
    small_recv,
    piece_send,
    piece_recv,
    mask_send,
    mask_recv,
):
    me = lax.axis_index("rows")
    rois = sent.shape[0]
    band_rows, columns, chans = band.shape
    has_up = me > 0
    has_down = me < count - 1

    def at(step):
        return {"rows": lax.rem(me + step + count, count)}

    barrier = pltpu.get_barrier_semaphore()
    for step in range(1, WINDOW):
        for sign in (1, -1):
            pl.semaphore_signal(barrier, inc=1, device_id=at(sign * step), device_id_type=MESH)

    loads = [
        pltpu.make_async_copy(feat, band, load_sem.at[0]),
        pltpu.make_async_copy(fpn_hbm, fpn_w, load_sem.at[1]),
        pltpu.make_async_copy(head_hbm, head_w, load_sem.at[2]),
        pltpu.make_async_copy(dec_hbm, dec_w, load_sem.at[3]),
    ]
    for load in loads:
        load.start()

    halves = wide.shape[0]
    lanes = wide.shape[-1]
    wide[:, :, 0:EDGE, :] = jnp.zeros((halves, band_rows + 1, EDGE, lanes), jnp.float32)
    wide[:, :, EDGE + columns :, :] = jnp.zeros((halves, band_rows + 1, EDGE, lanes), jnp.float32)
    blocks[...] = jnp.zeros_like(blocks)

    pl.semaphore_wait(barrier, 2 * (WINDOW - 1))

    corners_up = pltpu.make_async_remote_copy(
        src_ref=corners_vm,
        dst_ref=near_vm,
        send_sem=small_send.at[0],
        recv_sem=small_recv.at[0],
        device_id=at(1),
        device_id_type=MESH,
    )
    last_row = pltpu.make_async_remote_copy(
        src_ref=feat.at[pl.ds(band_rows - 1, 1)],
        dst_ref=above_row,
        send_sem=small_send.at[1],
        recv_sem=small_recv.at[1],
        device_id=at(1),
        device_id_type=MESH,
    )

    @pl.when(has_down)
    def _():
        corners_up.start()
        last_row.start()

    loads[0].wait()

    def widen(i, carry):
        for h in range(halves):
            wide[h, pl.ds(i + 1, 1), EDGE : EDGE + columns, :] = band[
                pl.ds(i, 1), :, h * lanes : (h + 1) * lanes
            ].astype(jnp.float32)
        return carry

    lax.fori_loop(0, band_rows, widen, 0)

    def piece(q):
        return pltpu.make_async_remote_copy(
            src_ref=sent.at[q],
            dst_ref=got.at[q],
            send_sem=piece_send.at[q],
            recv_sem=piece_recv.at[q],
            device_id=at(-1),
            device_id_type=MESH,
        )

    @pl.when(has_up)
    def _():
        last_row.wait_recv()
        for h in range(halves):
            wide[h, 0:1, EDGE : EDGE + columns, :] = above_row[
                :, :, h * lanes : (h + 1) * lanes
            ].astype(jnp.float32)
        corners_up.wait_recv()
        near = pltpu.make_async_copy(near_vm, near_sm, load_sem.at[4])
        near.start()
        near.wait()

        def gather(q, carry):
            start = near_sm[1, q] + (EDGE - 1)
            for h in range(halves):
                part = slice(h * lanes, (h + 1) * lanes)
                for i in range(band_rows):
                    sent[q, i, :, part] = wide[h, i + 1, pl.ds(start + 1, SIDE), :].astype(
                        jnp.bfloat16
                    )
                    ends[0, i : i + 1, part] = wide[h, i + 1, pl.ds(start, 1), :]
                    ends[1, i : i + 1, part] = wide[h, i + 1, pl.ds(start + SIDE + 1, 1), :]
            sent[q, SIDE:] = ends[...].astype(jnp.bfloat16)
            piece(q).start()
            return carry

        lax.fori_loop(0, rois, gather, 0)

    @pl.when(jnp.logical_not(has_up))
    def _():
        wide[:, 0:1, EDGE : EDGE + columns, :] = jnp.zeros((halves, 1, columns, lanes), jnp.float32)

    def own(q, carry):
        start = corners_sm[1, q] + (EDGE - 1)
        for dj in range(3):
            for h in range(halves):
                for i in range(band_rows + 1):
                    wins[q, dj, i, :, h * lanes : (h + 1) * lanes] = wide[
                        h, i, pl.ds(start + dj, SIDE), :
                    ].astype(jnp.bfloat16)
        return carry

    lax.fori_loop(0, rois, own, 0)

    @pl.when(jnp.logical_not(has_down))
    def _():
        got[...] = jnp.zeros_like(got)

    for load in loads[1:]:
        load.wait()

    limit = jnp.where(has_down, 2 * band_rows, band_rows)

    def group(g, carry):
        base = g * GROUP
        for u in range(GROUP):
            q = base + u

            @pl.when(has_down)
            def _():
                piece(q).wait_recv()

            joined[:, 8 : 8 + SIDE, :] = got[q, 0:SIDE].astype(jnp.float32)
            ends[...] = got[q, SIDE:].astype(jnp.float32)
            for i in range(band_rows):
                joined[i, 7:8, :] = ends[0, i : i + 1, :]
                joined[i, 8 + SIDE : 9 + SIDE, :] = ends[1, i : i + 1, :]
            for dj in range(3):
                wins[q, dj, band_rows + 1 :] = joined[:, 7 + dj : 7 + dj + SIDE, :].astype(
                    jnp.bfloat16
                )
        tops = [lax.rem(corners_sm[0, base + u], band_rows) for u in range(GROUP)]
        total = None
        for tap in range(9):
            di, dj = tap // 3, tap % 3
            lhs = jnp.concatenate(
                [
                    wins[base + u, dj, pl.ds(tops[u] + di, SIDE)].reshape(SIDE * SIDE, chans)
                    for u in range(GROUP)
                ],
                axis=0,
            )
            term = jnp.dot(
                lhs, fpn_w[tap * chans : (tap + 1) * chans], preferred_element_type=jnp.float32
            )
            total = term if total is None else total + term
        total = total.reshape(GROUP, SIDE, SIDE, chans)
        row = lax.broadcasted_iota(jnp.int32, (SIDE, SIDE, chans), 0)
        for u in range(GROUP):
            kept = jnp.where(row + tops[u] < limit, total[u], 0.0)
            blocks[u, 1 : 1 + SIDE, 8 : 8 + SIDE, :] = kept
        total = None
        for tap in range(9):
            di, dj = tap // 3, tap % 3
            lhs = (
                blocks[:, di : di + SIDE, 7 + dj : 7 + dj + SIDE, :]
                .astype(jnp.bfloat16)
                .reshape(GROUP * SIDE * SIDE, chans)
            )
            term = jnp.dot(
                lhs, head_w[tap * chans : (tap + 1) * chans], preferred_element_type=jnp.float32
            )
            total = term if total is None else total + term
        hidden = jnp.maximum(total, 0.0).astype(jnp.bfloat16)
        for yx in range(4):
            up = jnp.dot(
                hidden, dec_w[:, yx * chans : (yx + 1) * chans], preferred_element_type=jnp.float32
            )
            up = jnp.maximum(up, 0.0).astype(jnp.bfloat16)
            every = lax.dot_general(
                cls_w[...], up, (((1,), (1,)), ((), ())), preferred_element_type=jnp.float32
            )
            which = lax.broadcasted_iota(jnp.int32, (every.shape[0], SIDE * SIDE), 0)
            for u in range(GROUP):
                mine = every[:, u * SIDE * SIDE : (u + 1) * SIDE * SIDE]
                logits[base + u, yx : yx + 1, :] = jnp.sum(
                    jnp.where(which == class_sm[base + u], mine, 0.0), axis=0, keepdims=True
                )
        return carry

    lax.fori_loop(0, rois // GROUP, group, 0)

    slots = []
    for q in range(rois):
        rank = jnp.int32(0)
        for p in range(q):
            same = (offset_sm[p] == offset_sm[q]) & (p < count_sm[0])
            rank = rank + same.astype(jnp.int32)
        slots.append(jnp.where(q < count_sm[0], offset_sm[q] * SLOTS + rank, WINDOW * SLOTS))

    def mask(f):
        return pltpu.make_async_remote_copy(
            src_ref=outgoing.at[f],
            dst_ref=incoming.at[f],
            send_sem=mask_send.at[f],
            recv_sem=mask_recv.at[f],
            device_id=at(f),
            device_id_type=MESH,
        )

    for f in range(WINDOW - 1, -1, -1):
        for k in range(SLOTS):
            held = jnp.zeros(logits.shape[1:], jnp.float32)
            for q in range(rois):
                held = jnp.where(slots[q] == f * SLOTS + k, logits[q], held)
            if f:
                outgoing[f, k] = held
            else:
                out[k] = held
        if f:
            mask(f).start()

    for f in range(1, WINDOW):
        mask(f).wait_recv()
        out[f * SLOTS : (f + 1) * SLOTS] = incoming[f]

    for f in range(1, WINDOW):
        mask(f).wait_send()

    @pl.when(has_down)
    def _():
        corners_up.wait_send()
        last_row.wait_send()

    @pl.when(has_up)
    def _():
        def drain(q, carry):
            piece(q).wait_send()
            return carry

        lax.fori_loop(0, rois, drain, 0)


def body(
    count,
    features,
    corners,
    offsets,
    counts,
    classes,
    fpn_weight,
    head_weight,
    deconv_weight,
    class_weight,
):
    band_rows, columns, chans = features.shape
    rois = corners.shape[0]
    spots = corners.T
    smem = pl.BlockSpec(memory_space=pltpu.SMEM)
    cls = class_weight
    vmem = pl.BlockSpec(memory_space=pltpu.VMEM)
    anyw = pl.BlockSpec(memory_space=pl.ANY)
    bf16, f32 = jnp.bfloat16, jnp.float32
    cells = SIDE * SIDE
    masks = pl.pallas_call(
        functools.partial(kernel, count),
        out_shape=jax.ShapeDtypeStruct((WINDOW * SLOTS, 4, cells), f32),
        in_specs=[smem, vmem, smem, smem, smem, anyw, anyw, anyw, anyw, vmem],
        out_specs=vmem,
        scratch_shapes=[
            pltpu.VMEM(features.shape, bf16),
            pltpu.VMEM((chans // 128, band_rows + 1, columns + 2 * EDGE, 128), f32),
            pltpu.VMEM(fpn_weight.shape, bf16),
            pltpu.VMEM(head_weight.shape, bf16),
            pltpu.VMEM(deconv_weight.shape, bf16),
            pltpu.VMEM((1, columns, chans), bf16),
            pltpu.VMEM(spots.shape, jnp.int32),
            pltpu.SMEM(spots.shape, jnp.int32),
            pltpu.VMEM((rois, SIDE + 2, SIDE, chans), bf16),
            pltpu.VMEM((rois, SIDE + 2, SIDE, chans), bf16),
            pltpu.VMEM((2, SIDE, chans), f32),
            pltpu.VMEM((SIDE, 2 * SIDE, chans), f32),
            pltpu.VMEM((rois, 3, 2 * band_rows + 1, SIDE, chans), bf16),
            pltpu.VMEM((GROUP, SIDE + 2, 2 * SIDE, chans), f32),
            pltpu.VMEM((rois, 4, cells), f32),
            pltpu.VMEM((WINDOW, SLOTS, 4, cells), f32),
            pltpu.VMEM((WINDOW, SLOTS, 4, cells), f32),
            pltpu.SemaphoreType.DMA((5,)),
            pltpu.SemaphoreType.DMA((2,)),
            pltpu.SemaphoreType.DMA((2,)),
            pltpu.SemaphoreType.DMA((rois,)),
            pltpu.SemaphoreType.DMA((rois,)),
            pltpu.SemaphoreType.DMA((WINDOW,)),
            pltpu.SemaphoreType.DMA((WINDOW,)),
        ],
        compiler_params=pltpu.CompilerParams(collective_id=0, has_side_effects=True),
    )(
        spots,
        spots,
        offsets.reshape(rois),
        counts,
        classes,
        features,
        fpn_weight,
        head_weight,
        deconv_weight,
        cls,
    )
    masks = masks.reshape(WINDOW * SLOTS, 2, 2, SIDE, SIDE)
    return masks.transpose(0, 3, 1, 4, 2).reshape(WINDOW * SLOTS, 4 * cells)


def solution(mesh):
    placed = (
        P(("tiles", "rows"), None, None),
        P(("tiles", "rows"), None),
        P(("tiles", "rows"), None),
        P(("tiles", "rows")),
        P(("tiles", "rows")),
        P(),
        P(),
        P(),
        P(),
    )
    return jax.shard_map(
        functools.partial(body, mesh.shape["rows"]),
        mesh=mesh,
        in_specs=placed,
        out_specs=P(("tiles", "rows"), None),
        check_vma=False,
    )
```
